32 devices in a mesh: ev: 4 (over y, x), co: 8 (over z, core).
Axes of the slice: x: 2, y: 2, z: 4, core: 2. Of those that a mesh axis runs over, the one named last changes fastest.
Arguments:
- eval_points: float32 [2048, 1024], P('ev', 'co'), may hold values from -7 to 7
- corpus_points: float32 [4096, 1024], P('co', 'ev'), may hold values from -7 to 7
Outputs:
- eval_mapped: float32 [2048, 1024], P(('ev', 'co'))
- corpus_mapped: float32 [4096, 1024], P(('co', 'ev'))
- eval_potential: float32 [2048], P('ev')
- corpus_potential: float32 [4096], P('co')
The draws below stay inside these ranges and needn't reach their ends.
All inputs are finite; a program needn't handle non-finite values.
Results may differ from the reference program's by a relative error of at most 0.0003.
Values sent between devices are 32-bit elements; how exact they have to be, the bound alone decides.
No kernel may reach another device: no remote copies, remote signals or barrier semaphores. Data moves between devices by JAX's collectives and lax.ppermute only.
A program may use at most 64 MiB of HBM per device.

```python
import math
import jax
import jax.numpy as jnp
from jax import lax

D = 1024
XR = 512
ITERS = 3
NX = 2048
NY = 4096


def paired_points(key):
    keys = jax.random.split(jax.random.fold_in(key, 4111), 9)
    eval_base = jax.random.normal(keys[0], (NX, D), jnp.float32)
    corpus_base = jax.random.normal(keys[1], (NY, D), jnp.float32)
    eval_scale = jnp.exp(jax.random.uniform(keys[2], (NX, 1), jnp.float32, math.log(0.5), math.log(2.5)))
    corpus_scale = jnp.exp(jax.random.uniform(keys[3], (NY, 1), jnp.float32, math.log(0.5), math.log(2.5)))
    corpus_drawn = corpus_base * corpus_scale
    half = NY // 2
    first_half = corpus_drawn[:half]
    second_half = corpus_drawn[half:]
    twin_mask = jax.random.randint(keys[4], (half, 1), 0, 2) == 0
    twin_rows = first_half + 0.2 * jax.random.normal(keys[5], (half, D), jnp.float32)
    corpus_all = jnp.concatenate([first_half, jnp.where(twin_mask, twin_rows, second_half)], axis=0)
    partner = jax.random.randint(keys[6], (NX,), 0, NY)
    copy_mask = jax.random.randint(keys[7], (NX, 1), 0, 4) == 0
    near_rows = corpus_all[partner] + 0.1 * jax.random.normal(keys[8], (NX, D), jnp.float32)
    eval_all = jnp.where(copy_mask, near_rows, eval_base * eval_scale)
    return (jnp.clip(eval_all, -7.0, 7.0), jnp.clip(corpus_all, -7.0, 7.0))


def draw_eval_points(key, part):
    return paired_points(key)[0]


def draw_corpus_points(key, part):
    return paired_points(key)[1]


def setup_inputs(seed: int = 0) -> dict:
    streams_of = jax.random.split(jax.random.key(seed), 3)
    return {
        "eval_points": draw_eval_points(jax.random.fold_in(streams_of[2], 71), 0),
        "corpus_points": draw_corpus_points(jax.random.fold_in(streams_of[2], 71), 0),
    }


EPSILON = 0.02


def lse_along(scores, along):
    largest = jnp.max(scores, axis=along, keepdims=True)
    summed = jnp.sum(jnp.exp(scores - largest), axis=along, keepdims=True)
    return jnp.squeeze(largest + jnp.log(summed), axis=along)


def reference(eval_points, corpus_points):
    corpus_norms = jnp.sum(corpus_points * corpus_points, axis=1)

    def cost_rows(eval_block):
        block_norms = jnp.sum(eval_block * eval_block, axis=1)
        cross_term = jnp.dot(eval_block, corpus_points.T, precision=lax.Precision.HIGHEST, preferred_element_type=jnp.float32)
        return (block_norms[:, None] + corpus_norms[None, :] - 2.0 * cross_term) / D

    blocks = eval_points.reshape(NX // XR, XR, D)
    cost_tile = lax.map(cost_rows, blocks).reshape(NX, NY)
    log_mass_x = -jnp.log(jnp.float32(NX))
    log_mass_y = -jnp.log(jnp.float32(NY))
    corpus_potential = jnp.zeros((NY,), jnp.float32)
    eval_potential = jnp.zeros((NX,), jnp.float32)
    column_lse = jnp.zeros((NY,), jnp.float32)
    for sweep in range(ITERS):
        eval_potential = EPSILON * log_mass_x - EPSILON * lse_along((corpus_potential[None, :] - cost_tile) / EPSILON, 1)
        column_lse = lse_along((eval_potential[:, None] - cost_tile) / EPSILON, 0)
        corpus_potential = EPSILON * log_mass_y - EPSILON * column_lse
    row_scores = (corpus_potential[None, :] - cost_tile) / EPSILON
    row_final = lse_along(row_scores, 1)
    x_weights = jnp.exp(row_scores - row_final[:, None])
    eval_mapped = jnp.dot(x_weights, corpus_points, precision=lax.Precision.HIGHEST, preferred_element_type=jnp.float32)
    y_weights = jnp.exp((eval_potential[:, None] - cost_tile) / EPSILON - column_lse[None, :])
    corpus_mapped = jnp.dot(y_weights.T, eval_points, precision=lax.Precision.HIGHEST, preferred_element_type=jnp.float32)
    return (eval_mapped, corpus_mapped, eval_potential, corpus_potential)
```

```python
import math

import jax
import jax.numpy as jnp
from jax import lax
from jax.sharding import PartitionSpec as P

ITERS = 3
EPSILON = 0.02
CHUNKS = 2
HIGHEST = lax.Precision.HIGHEST


def xor_pairs(size, mask):
    return [(i, i ^ mask) for i in range(size)]


def radix_groups(size, first_bit=0):
    bits = [1 << b for b in range(first_bit, size.bit_length() - 1)]
    return [bits[i : i + 2] for i in range(0, len(bits), 2)]


def exchange(value, axis, group):
    size = lax.axis_size(axis)
    if len(group) == 1:
        return [value, lax.ppermute(value, axis, xor_pairs(size, group[0]))]
    low, high = group
    return [value] + [
        lax.ppermute(value, axis, xor_pairs(size, mask)) for mask in (low, high, low | high)
    ]


def tree(values, add):
    while len(values) > 1:
        values = [add(values[i], values[i + 1]) for i in range(0, len(values), 2)]
    return values[0]


def groups_of(axis):
    size = lax.axis_size(axis)
    return [[1]] + radix_groups(size, 1) if axis == "co" else radix_groups(size)


def sum_over(value, axis):
    for group in groups_of(axis):
        value = tree(exchange(value, axis, group), jnp.add)
    return value


def lse_over(largest, summed, axis):
    for group in groups_of(axis):
        pairs = exchange(jnp.stack([largest, summed]), axis, group)
        top = tree([pair[0] for pair in pairs], jnp.maximum)
        summed = tree([pair[1] * jnp.exp(pair[0] - top) for pair in pairs], jnp.add)
        largest = top
    return largest, summed


def line_pairs(lines, step, carried):
    if carried:
        up, down = (lambda z: z <= step), (lambda z: z >= lines - 1 - step)
    else:
        up, down = (lambda z: z >= step), (lambda z: z + step < lines)
    return [(2 * z, 2 * z + 2) for z in range(lines - 1) if up(z)] + [
        (2 * z + 1, 2 * z - 1) for z in range(1, lines) if down(z)
    ]


def gather_over_co(block):
    size = lax.axis_size("co")
    lines = size // 2
    z, core = lax.axis_index("co") // 2, lax.axis_index("co") % 2
    swap = xor_pairs(size, 1)
    other = lax.ppermute(block, "co", swap)
    chip = jnp.where(
        core == 0, jnp.concatenate([block, other], 1), jnp.concatenate([other, block], 1)
    )
    whole = jnp.zeros((lines + 1,) + chip.shape, chip.dtype)
    whole = lax.dynamic_update_index_in_dim(whole, chip, z, 0)
    moving = chip
    for step in range(lines - 1):
        moving = lax.ppermute(moving, "co", line_pairs(lines, step, False))
        swapped = lax.ppermute(moving, "co", swap)
        below, above = z - 1 - step, z + 1 + step
        below = jnp.where(below >= 0, below, lines)
        above = jnp.where(above < lines, above, lines)
        whole = lax.dynamic_update_index_in_dim(
            whole, moving, jnp.where(core == 0, below, above), 0
        )
        whole = lax.dynamic_update_index_in_dim(
            whole, swapped, jnp.where(core == 0, above, below), 0
        )
    return whole


def gather_over_ev(block, order):
    size = lax.axis_size("ev")
    me = lax.axis_index("ev")
    whole = jnp.zeros((size,) + block.shape, block.dtype)
    whole = lax.dynamic_update_index_in_dim(whole, block, me, 0)
    held = [(0, block)]
    for bit in order:
        sent = jnp.stack([b for _, b in held]) if len(held) > 1 else held[0][1][None]
        got = lax.ppermute(sent, "ev", xor_pairs(size, bit))
        new = [(mask | bit, got[i]) for i, (mask, _) in enumerate(held)]
        for mask, b in new:
            whole = lax.dynamic_update_index_in_dim(whole, b, me ^ mask, 0)
        held = held + new
    return whole


def scatter_over_ev(part, order):
    size = lax.axis_size("ev")
    me = lax.axis_index("ev")
    count = size.bit_length() - 1
    part = part.reshape((2,) * count + part.shape[1:])
    left = [1 << b for b in reversed(range(count))]
    for bit in order:
        axis = left.index(bit)
        mine = ((me & bit) != 0).astype(jnp.int32)
        sent = lax.dynamic_index_in_dim(part, 1 - mine, axis, False)
        kept = lax.dynamic_index_in_dim(part, mine, axis, False)
        part = kept + lax.ppermute(sent, "ev", xor_pairs(size, bit))
        left.pop(axis)
    return part


def scatter_over_co(part):
    size = lax.axis_size("co")
    lines = size // 2
    z, core = lax.axis_index("co") // 2, lax.axis_index("co") % 2
    arrived = None
    for step in range(lines - 1):
        away = lines - 1 - step
        up, down = jnp.clip(z + away, 0, lines - 1), jnp.clip(z - away, 0, lines - 1)
        own = jnp.where(core == 0, up, down)
        swap = [(2 * q + 1, 2 * q) for q in range(lines - 1) if q <= step] + [
            (2 * q, 2 * q + 1) for q in range(1, lines) if q >= away
        ]
        given = lax.ppermute(
            lax.dynamic_index_in_dim(part, jnp.where(core == 0, down, up), 0, False), "co", swap
        )
        moving = lax.dynamic_index_in_dim(part, own, 0, False) + given
        if arrived is not None:
            moving = moving + arrived
        arrived = lax.ppermute(moving, "co", line_pairs(lines, step, True))
    last = lax.dynamic_index_in_dim(part, z, 0, False) + arrived
    given = lax.ppermute(
        lax.dynamic_index_in_dim(last, 1 - core, 0, False), "co", xor_pairs(size, 1)
    )
    return lax.dynamic_index_in_dim(last, core, 0, False) + given


def dot(left, right, left_dim, right_dim):
    return lax.dot_general(
        left,
        right,
        (((left_dim,), (right_dim,)), ((), ())),
        precision=HIGHEST,
        preferred_element_type=jnp.float32,
    )


def on_device(eval_points, corpus_points):
    ev, co = lax.axis_size("ev"), lax.axis_size("co")
    lines = co // 2
    rows, columns = eval_points.shape[0], corpus_points.shape[0]
    width = eval_points.shape[1] * co
    log_mass_x, log_mass_y = math.log(rows * ev), math.log(columns * co)
    masks = [1 << b for b in range(ev.bit_length() - 1)]

    step = rows // CHUNKS
    eval_blocks = [
        gather_over_co(eval_points[c * step : (c + 1) * step]) for c in range(CHUNKS)
    ]
    half = columns // 2
    corpus_blocks = [
        gather_over_ev(corpus_points[:half], masks),
        gather_over_ev(corpus_points[half:], masks[::-1]),
    ]
    eval_full = jnp.concatenate([b[:lines] for b in eval_blocks], 1)
    corpus_full = jnp.concatenate(corpus_blocks, 1)
    if lines != ev:
        eval_full = jnp.concatenate(list(eval_full), 1)[None]
        corpus_full = jnp.concatenate(list(corpus_full), 1)[None]
    blocks = eval_full.shape[0]

    eval_norms = jnp.sum(eval_full * eval_full, axis=(0, 2))
    corpus_norms = jnp.sum(corpus_full * corpus_full, axis=(0, 2))
    cross = dot(eval_full[0], corpus_full[0], 1, 1)
    for b in range(1, blocks):
        cross = cross + dot(eval_full[b], corpus_full[b], 1, 1)
    cost = (eval_norms[:, None] + corpus_norms[None, :] - 2.0 * cross) / width

    scores = cost * (-1.0 / EPSILON)
    top = jnp.max(scores, axis=1)
    top, total = lse_over(top, jnp.sum(jnp.exp(scores - top[:, None]), axis=1), "co")
    eval_log = -log_mass_x - (top + jnp.log(total))
    scores = scores + eval_log[:, None]
    near = jnp.max(scores, axis=0)
    plan = jnp.exp(scores - near[None, :])
    top, total = lse_over(near, jnp.sum(plan, axis=0), "ev")
    corpus_log = -log_mass_y - (top + jnp.log(total))
    plan = plan * jnp.exp(near + corpus_log)[None, :]

    corpus_scale = jnp.ones((columns,), jnp.float32)
    for sweep in range(1, ITERS):
        row_sum = sum_over(jnp.sum(plan * corpus_scale[None, :], axis=1), "co")
        eval_scale = 1.0 / (row_sum * (rows * ev))
        y_weights = plan * eval_scale[:, None]
        column_sum = sum_over(jnp.sum(y_weights, axis=0), "ev")
        corpus_scale = 1.0 / (column_sum * (columns * co))
    eval_potential = EPSILON * (eval_log + jnp.log(eval_scale))
    corpus_potential = EPSILON * (corpus_log + jnp.log(corpus_scale))

    x_weights = plan * corpus_scale[None, :]
    row_sum = sum_over(jnp.sum(x_weights, axis=1), "co")
    eval_portion, corpus_portion = rows // co, columns // ev

    def mapped(weights, dims, full, scatter, shape):
        pieces = []
        for c in range(CHUNKS):
            span = blocks // CHUNKS if blocks > 1 else 1
            group = [full[b] for b in range(c * span, (c + 1) * span)]
            if blocks == 1:
                part = full.shape[2] // CHUNKS
                group = [full[0, :, c * part : (c + 1) * part]]
            product = jnp.concatenate([dot(weights, g, dims, 0) for g in group], 1)
            pieces.append(scatter(product.reshape(shape + (product.shape[1],)), c))
        return jnp.concatenate(pieces, 1)

    corpus_mapped = mapped(
        y_weights,
        0,
        eval_full,
        lambda part, c: scatter_over_ev(part, masks if c % 2 == 0 else masks[::-1]),
        (ev, corpus_portion),
    )
    eval_mapped = mapped(
        x_weights, 1, corpus_full, lambda part, c: scatter_over_co(part), (lines, 2, eval_portion)
    )
    row_here = lax.dynamic_slice_in_dim(
        row_sum, lax.axis_index("co") * eval_portion, eval_portion, 0
    )
    column_here = lax.dynamic_slice_in_dim(
        column_sum, lax.axis_index("ev") * corpus_portion, corpus_portion, 0
    )
    return (
        eval_mapped / row_here[:, None],
        corpus_mapped / column_here[:, None],
        eval_potential,
        corpus_potential,
    )


def solution(mesh):
    return jax.shard_map(
        on_device,
        mesh=mesh,
        in_specs=(P("ev", "co"), P("co", "ev")),
        out_specs=(P(("ev", "co"), None), P(("co", "ev"), None), P("ev"), P("co")),
        check_vma=False,
    )
```

```python
import math

import jax
import jax.numpy as jnp
from jax import lax
from jax.experimental import pallas as pl
from jax.experimental.pallas import tpu as pltpu
from jax.sharding import PartitionSpec as P

ITERS = 3
EPSILON = 0.02
CHUNKS = 2
VMEM_LIMIT = 12 << 20
LANES = 128


def xor_pairs(size, mask):
    return [(i, i ^ mask) for i in range(size)]


def radix_groups(size, first_bit=0):
    bits = [1 << b for b in range(first_bit, size.bit_length() - 1)]
    return [bits[i : i + 2] for i in range(0, len(bits), 2)]


def exchange(value, axis, group):
    size = lax.axis_size(axis)
    if len(group) == 1:
        return [value, lax.ppermute(value, axis, xor_pairs(size, group[0]))]
    low, high = group
    return [value] + [
        lax.ppermute(value, axis, xor_pairs(size, mask)) for mask in (low, high, low | high)
    ]


def tree(values, add):
    while len(values) > 1:
        values = [add(values[i], values[i + 1]) for i in range(0, len(values), 2)]
    return values[0]


def groups_of(axis):
    size = lax.axis_size(axis)
    return [[1]] + radix_groups(size, 1) if axis == "co" else radix_groups(size)


def sum_over(value, axis, skip=0):
    for group in groups_of(axis)[skip:]:
        value = tree(exchange(value, axis, group), jnp.add)
    return value


def lse_over(largest, summed, axis):
    for group in groups_of(axis):
        pairs = exchange(jnp.stack([largest, summed]), axis, group)
        top = tree([pair[0] for pair in pairs], jnp.maximum)
        summed = tree([pair[1] * jnp.exp(pair[0] - top) for pair in pairs], jnp.add)
        largest = top
    return largest, summed


def xor_gather(block, axis, shift, lines):
    size = lax.axis_size(axis)

    def send(value, mask):
        return lax.ppermute(value, axis, xor_pairs(size, mask << shift))

    if lines == 4:
        high, low = send(block, 2), send(block, 1)
        return {0: block, 1: low, 2: high, 3: (high, low)}, send
    parts = {0: block}
    bit = 1
    while bit < lines:
        masks = list(parts)
        got = send(jnp.stack([parts[m] for m in masks]), bit)
        parts.update({m | bit: got[i] for i, m in enumerate(masks)})
        bit *= 2
    return parts, send


def gather_over_co(block):
    size = lax.axis_size("co")
    lines = size // 2
    z, core = lax.axis_index("co") // 2, lax.axis_index("co") % 2
    parts, send = xor_gather(block, "co", 1, lines)
    if lines == 4:
        parts[3] = send(parts[2], 1)
    pairs = {m: [p, lax.ppermute(p, "co", xor_pairs(size, 1))] for m, p in parts.items()}
    if block.shape[1] % LANES == 0:
        return [(z ^ m, pair) for m, pair in pairs.items()]
    whole = jnp.zeros((lines, 2) + block.shape, block.dtype)
    for mask, pair in pairs.items():
        chip = jnp.stack([jnp.where(core == k, pair[0], pair[1]) for k in range(2)])
        whole = lax.dynamic_update_index_in_dim(whole, chip, z ^ mask, 0)
    whole = whole.transpose(2, 0, 1, 3).reshape(block.shape[0], -1)
    return [(0, [whole])]


def gather_over_ev(block):
    size = lax.axis_size("ev")
    me = lax.axis_index("ev")
    half = block.shape[0] // 2
    parts, send = xor_gather(block, "ev", 0, size)
    parts = {m: [p] for m, p in parts.items()}
    if size == 4:
        parts[3] = [send(parts[1][0][:half], 2), send(parts[2][0][half:], 1)]
    if block.shape[1] % LANES == 0:
        return [(me ^ m, p) for m, p in parts.items()]
    whole = jnp.zeros((size,) + block.shape, block.dtype)
    for mask, part in parts.items():
        whole = lax.dynamic_update_index_in_dim(whole, jnp.concatenate(part, 0), me ^ mask, 0)
    return [(0, [whole.transpose(1, 0, 2).reshape(block.shape[0], -1)])]


def halve(pieces, order, send):
    for bit in order:
        moved = [m for m in pieces if m & bit]
        rows = pieces[moved[0]].shape[0]
        got = send(jnp.concatenate([pieces[m] for m in moved], 0), bit)
        pieces = {m: p for m, p in pieces.items() if not m & bit}
        for i, m in enumerate(moved):
            pieces[m ^ bit] = pieces[m ^ bit] + got[i * rows : (i + 1) * rows]
    return pieces[0]


def relative(parts, count, me):
    rows = parts.shape[0] // count
    return {m: lax.dynamic_slice_in_dim(parts, (me ^ m) * rows, rows, 0) for m in range(count)}


def scatter_over_ev(chunks):
    size = lax.axis_size("ev")
    me = lax.axis_index("ev")
    bits = [1 << b for b in range(size.bit_length() - 1)]

    def send(value, mask):
        return lax.ppermute(value, "ev", xor_pairs(size, mask))

    return jnp.concatenate(
        [
            halve(relative(part, size, me), bits if c % 2 == 0 else bits[::-1], send)
            for c, part in enumerate(chunks)
        ],
        1,
    )


def scatter_over_co(chunks):
    size = lax.axis_size("co")
    lines = size // 2
    z = lax.axis_index("co") // 2

    def send(value, mask):
        return lax.ppermute(value, "co", xor_pairs(size, 2 * mask))

    pieces = [relative(part, lines, z) for part in chunks]
    if lines != 4:
        bits = [1 << b for b in range(lines.bit_length() - 1)]
        return jnp.concatenate([halve(p, bits, send) for p in pieces], 1)
    relayed = [send(p[3], 1) for p in pieces]
    far = [send(p[2] + r, 2) for p, r in zip(pieces, relayed)]
    near = send(jnp.concatenate([p[1] for p in pieces], 1), 1)
    return jnp.concatenate([p[0] + f for p, f in zip(pieces, far)], 1) + near


def whole_call(body, outs, flops, *args, scalars=None, scratch=()):
    moved = sum(math.prod(a.shape) * a.dtype.itemsize for a in (*args, *outs))
    vmem = pl.BlockSpec(memory_space=pltpu.VMEM)
    specs = [vmem] * len(args)
    if scalars is not None:
        specs = [pl.BlockSpec(memory_space=pltpu.SMEM)] + specs
        args = (scalars, *args)
    return pl.pallas_call(
        body,
        out_shape=outs,
        in_specs=specs,
        out_specs=(vmem,) * len(outs),
        scratch_shapes=scratch,
        cost_estimate=pl.CostEstimate(flops=flops, bytes_accessed=moved, transcendentals=0),
        compiler_params=pltpu.CompilerParams(vmem_limit_bytes=VMEM_LIMIT),
    )(*args)


def pieces_of(value, count):
    terms = []
    for _ in range(count):
        terms.append(value.astype(jnp.bfloat16))
        value = value - terms[-1].astype(jnp.float32)
    return terms


def score_tile(eval_parts, corpus_parts, norms, scale):
    width = sum(p.shape[1] for _, pair in eval_parts for p in pair)
    slots = jnp.stack(
        [lax.axis_index("co") % 2]
        + [jnp.asarray(slot, jnp.int32) for slot, _ in eval_parts + corpus_parts]
    ).astype(jnp.int32)
    flat = [p for _, pair in eval_parts + corpus_parts for p in pair]
    rows = eval_parts[0][1][0].shape[0]
    columns = sum(p.shape[0] for p in corpus_parts[0][1])

    def body(slot_ref, *refs):
        inputs, norm_ref = refs[: len(flat)], refs[len(flat)]
        score_ref, eh, em, ch, cm, el, cl = refs[len(flat) + 1 :]
        at = 0
        for k, (_, pair) in enumerate(eval_parts):
            blocks = [inputs[at + i][...] for i in range(len(pair))]
            at += len(pair)
            if len(blocks) == 2:
                first = slot_ref[0] == 0
                blocks = [
                    jnp.where(first, blocks[0], blocks[1]),
                    jnp.where(first, blocks[1], blocks[0]),
                ]
            wide = sum(b.shape[1] for b in blocks)
            start = 0
            for block in blocks:
                place = slot_ref[1 + k] * wide + start
                start += block.shape[1]
                place = pl.ds(pl.multiple_of(place, LANES), block.shape[1])
                for ref, term in zip((eh, em, el), pieces_of(block, 3)):
                    ref[:, place] = term
        for k, (_, pair) in enumerate(corpus_parts):
            row = 0
            for i in range(len(pair)):
                block = inputs[at + i]
                place = slot_ref[1 + len(eval_parts) + k] * block.shape[1]
                place = pl.ds(pl.multiple_of(place, LANES), block.shape[1])
                for ref, term in zip((ch, cm, cl), pieces_of(block[...], 3)):
                    ref[row : row + block.shape[0], place] = term
                row += block.shape[0]
            at += len(pair)

        def product(a, b):
            return lax.dot_general(
                a[...], b[...], (((1,), (1,)), ((), ())), preferred_element_type=jnp.float32
            )

        small = product(em, cm) + (product(eh, cl) + product(el, ch))
        cross = product(eh, ch) + ((product(eh, cm) + product(em, ch)) + small)
        score_ref[...] = (2.0 * cross - norm_ref[...]) * scale

    def term(n):
        return jax.ShapeDtypeStruct((n, width), jnp.bfloat16)

    return whole_call(
        body,
        (
            jax.ShapeDtypeStruct((rows, columns), jnp.float32),
            term(rows),
            term(rows),
            term(columns),
            term(columns),
        ),
        12 * rows * columns * width,
        *flat,
        norms,
        scalars=slots,
        scratch=(pltpu.VMEM((rows, width), jnp.bfloat16), pltpu.VMEM((columns, width), jnp.bfloat16)),
    )


def dot3(left, right, left_dim):
    def one(a, b):
        return lax.dot_general(
            a, b, (((left_dim,), (0,)), ((), ())), preferred_element_type=jnp.float32
        )

    return one(left[0], right[0]) + (one(left[0], right[1]) + one(left[1], right[0]))


def map_corpus(weights, terms):
    width = terms[0].shape[1] // CHUNKS

    def body(w_ref, high_ref, low_ref, *outs):
        left = pieces_of(w_ref[...], 2)
        for c, out in enumerate(outs):
            at = slice(c * width, (c + 1) * width)
            out[...] = dot3(left, (high_ref[:, at], low_ref[:, at]), 0)

    out = jax.ShapeDtypeStruct((weights.shape[1], width), jnp.float32)
    return whole_call(
        body, (out,) * CHUNKS, 6 * weights.size * width * CHUNKS, weights, *terms
    )


def map_eval(plans, scales, own_terms, pair_terms):
    width = own_terms[0].shape[1] // CHUNKS

    def body(own_ref, pair_ref, scale_ref, high_ref, low_ref, high2_ref, low2_ref, *outs):
        left = pieces_of(own_ref[...] * scale_ref[0:1, :], 2)
        left2 = pieces_of(pair_ref[...] * scale_ref[1:2, :], 2)
        for c, out in enumerate(outs):
            at = slice(c * width, (c + 1) * width)
            out[...] = dot3(left, (high_ref[:, at], low_ref[:, at]), 1) + dot3(
                left2, (high2_ref[:, at], low2_ref[:, at]), 1
            )

    out = jax.ShapeDtypeStruct((plans[0].shape[0], width), jnp.float32)
    return whole_call(
        body,
        (out,) * CHUNKS,
        12 * plans[0].size * width * CHUNKS,
        *plans,
        scales,
        *own_terms,
        *pair_terms,
    )


def split(parts):
    width = sum(pair[0].shape[1] for _, pair in parts)
    flat = [p for _, pair in parts for p in pair]
    rows = sum(p.shape[0] for p in parts[0][1])
    slots = jnp.stack([jnp.asarray(slot, jnp.int32) for slot, _ in parts]).astype(jnp.int32)

    def body(slot_ref, *refs):
        high, low = refs[len(flat) :]
        at = 0
        for k, (_, pair) in enumerate(parts):
            row = 0
            for _ in pair:
                block = refs[at]
                place = slot_ref[k] * block.shape[1]
                place = pl.ds(pl.multiple_of(place, LANES), block.shape[1])
                for ref, term in zip((high, low), pieces_of(block[...], 2)):
                    ref[row : row + block.shape[0], place] = term
                row += block.shape[0]
                at += 1

    out = jax.ShapeDtypeStruct((rows, width), jnp.bfloat16)
    return whole_call(body, (out, out), rows * width, *flat, scalars=slots)


def on_device(eval_points, corpus_points):
    ev, co = lax.axis_size("ev"), lax.axis_size("co")
    lines = co // 2
    rows, columns = eval_points.shape[0], corpus_points.shape[0]
    width = eval_points.shape[1] * co
    log_mass_x, log_mass_y = math.log(rows * ev), math.log(columns * co)
    swap = xor_pairs(co, 1)

    eval_parts = gather_over_co(eval_points)
    corpus_parts = gather_over_ev(corpus_points)
    corpus_pair = [
        (slot, [lax.ppermute(p, "co", swap) for p in part]) for slot, part in corpus_parts
    ]

    def squares(part, axis):
        return jnp.concatenate([jnp.sum(p * p, axis=1) for p in part], 0) if axis else sum(
            jnp.sum(p * p, axis=1) for p in part
        )

    corpus_norms = sum(squares(part, 1) for _, part in corpus_parts)
    scores, *terms = score_tile(
        eval_parts, corpus_parts, corpus_norms[None, :], 1.0 / (width * EPSILON)
    )
    eval_terms, corpus_terms = terms[:2], terms[2:]

    top = jnp.max(scores, axis=1)
    top, total = lse_over(top, jnp.sum(jnp.exp(scores - top[:, None]), axis=1), "co")
    eval_log = -log_mass_x - (top + jnp.log(total))
    scores = scores + eval_log[:, None]
    near = jnp.max(scores, axis=0)
    plan = jnp.exp(scores - near[None, :])
    plan_pair = lax.ppermute(plan, "co", swap)
    top, total = lse_over(near, jnp.sum(plan, axis=0), "ev")
    corpus_log = -log_mass_y - (top + jnp.log(total))
    factor = jnp.exp(near + corpus_log)
    factor_pair = lax.ppermute(factor, "co", swap)
    plan = plan * factor[None, :]
    plan_pair = plan_pair * factor_pair[None, :]

    row_sum = sum_over(jnp.sum(plan, axis=1), "co")
    for sweep in range(1, ITERS):
        eval_scale = 1.0 / (row_sum * (rows * ev))
        y_weights = plan * eval_scale[:, None]
        column_sums = jnp.stack(
            [jnp.sum(y_weights, axis=0), jnp.sum(plan_pair * eval_scale[:, None], axis=0)]
        )
        column_sums = sum_over(column_sums, "ev")
        corpus_scales = 1.0 / (column_sums * (columns * co))
        row_sum = jnp.sum(plan * corpus_scales[0][None, :], axis=1) + jnp.sum(
            plan_pair * corpus_scales[1][None, :], axis=1
        )
        row_sum = sum_over(row_sum, "co", 1)
    eval_norms = jnp.zeros((len(eval_parts), rows), jnp.float32)
    for slot, part in eval_parts:
        eval_norms = lax.dynamic_update_index_in_dim(eval_norms, squares(part, 0), slot, 0)
    eval_norms = jnp.sum(eval_norms, axis=0)
    eval_potential = EPSILON * (eval_log + jnp.log(eval_scale)) + eval_norms / width
    corpus_potential = EPSILON * (corpus_log + jnp.log(corpus_scales[0]))

    eval_portion, corpus_portion = rows // co, columns // ev

    corpus_mapped = scatter_over_ev(map_corpus(y_weights, eval_terms))
    core = lax.axis_index("co") % 2
    here = [
        lax.dynamic_index_in_dim(p.reshape(lines, 2, eval_portion, columns), core, 1, False)
        for p in (plan, plan_pair)
    ]
    eval_mapped = scatter_over_co(
        map_eval(
            [p.reshape(lines * eval_portion, columns) for p in here],
            corpus_scales,
            corpus_terms,
            split(corpus_pair),
        )
    )
    row_here = lax.dynamic_slice_in_dim(
        row_sum, lax.axis_index("co") * eval_portion, eval_portion, 0
    )
    column_here = lax.dynamic_slice_in_dim(
        column_sums[0], lax.axis_index("ev") * corpus_portion, corpus_portion, 0
    )
    return (
        eval_mapped / row_here[:, None],
        corpus_mapped / column_here[:, None],
        eval_potential,
        corpus_potential,
    )


def solution(mesh):
    return jax.shard_map(
        on_device,
        mesh=mesh,
        in_specs=(P("ev", "co"), P("co", "ev")),
        out_specs=(P(("ev", "co"), None), P(("co", "ev"), None), P("ev"), P("co")),
        check_vma=False,
    )
```
